128 devices in a mesh: pair: 2 (over core), row: 64 (over z, y, x).
Axes of the slice: x: 4, y: 4, z: 4, core: 2. Of those that a mesh axis runs over, the one named last changes fastest.
Arguments:
- snapshot: float32 [16384, 1024], P('row', 'pair'), may hold values from -6 to 6
- weights: float32 [8, 128], replicated, may hold values from 0 to 1
- block_home: int32 [8], P('pair'), may hold values from 0 to 7, each once
- plan: int32 [2, 2, 4], P(None, 'pair'), may hold values from 0 to 3, each once within a row
Outputs:
- rotated: float32 [16384, 1024], P('row', 'pair')
- column_norms: float32 [1024], P('pair')
The draws below stay inside these ranges and needn't reach their ends.
All inputs are finite; a program needn't handle non-finite values. Where the reference program divides by a largest or mean magnitude, that divisor is 1e-20 or more.
Results may differ from the reference program's by a relative error of at most 0.0001.
Values sent between devices are 32-bit elements; how exact they have to be, the bound alone decides.
A program may use at most 128 MiB of HBM per device.

```python
import jax
import jax.numpy as jnp
from jax import lax

B = 128
SLOTS = 4
ROUNDS = 2
NB = 8
N = 1024
M = 16384


def block_levels(key, extent, shards, low, top_value):
    def one(dim, blocks):
        steps = jax.random.uniform(jax.random.fold_in(jax.random.fold_in(key, 6), dim), (blocks,), jnp.float32, low / len(shards), top_value / len(shards))
        return jnp.repeat(jnp.exp(steps), extent[dim] // blocks).reshape((-1,) + (1,) * (len(extent) - dim - 1))

    gain = one(*shards[0])
    for cut in shards[1:]:
        gain = gain * one(*cut)
    return gain


def normal_values(key, extent, scale, bound, pieces=(), kind=jnp.bfloat16):
    values = jax.random.normal(key, extent, jnp.float32) * scale
    if len(pieces) > 0:
        values = block_levels(key, extent, pieces, -0.22, 0.18) * values
    return jnp.clip(values, min=-bound, max=bound).astype(kind)


def setup_inputs(seed: int = 0) -> dict:
    key_of = jax.random.split(jax.random.key(seed), 5)
    return {
        "snapshot": normal_values(key_of[0], (M, N), 1.0, 6.0, ((0, 64), (1, 2)), jnp.float32),
        "weights": jnp.clip(jax.random.uniform(key_of[1], (NB, B), jnp.float32, 0.0, 1.0), 0.0, 1.0),
        "block_home": jax.random.permutation(key_of[2], NB).astype(jnp.int32),
        "plan": jax.vmap(lambda own: jax.random.permutation(own, SLOTS))(jax.random.split(key_of[3], ROUNDS * (NB // SLOTS))).reshape((ROUNDS, NB // SLOTS, SLOTS)).astype(jnp.int32),
    }


epsilon = 1e-06
step_size = 4.0
newton_turns = 5
highest = lax.Precision.HIGHEST

def rotation(gram_matrix, spread):
    diagonal_part = jnp.diagonal(gram_matrix, axis1=1, axis2=2)
    inverse = lax.rsqrt(diagonal_part + epsilon)
    corr = gram_matrix * inverse[:, :, None] * inverse[:, None, :]
    skew_part = step_size * corr * (spread[:, :, None] - spread[:, None, :])
    row_bound = 1.0 + lax.optimization_barrier(jnp.max(lax.optimization_barrier(jnp.sum(jnp.abs(skew_part), axis=2)), axis=1))
    unit_matrix = jnp.eye(gram_matrix.shape[1], dtype=jnp.float32)
    current = unit_matrix[None] + skew_part / row_bound[:, None, None]
    for index in range(newton_turns):
        inner_gram = jnp.einsum('pcd,pce->pde', current, current, precision=highest)
        current = jnp.einsum('pcd,pde->pce', current, 1.5 * unit_matrix[None] - 0.5 * inner_gram, precision=highest)
    return current

def one_group(operands):
    blocks_here, scales = operands
    row_count = blocks_here.shape[0]
    paired = jnp.transpose(blocks_here.reshape(row_count, 2, 2 * B), (1, 0, 2))
    gram_matrix = jnp.einsum('prc,prd->pcd', paired, paired, precision=highest)
    turn_matrix = rotation(gram_matrix, scales.reshape(2, 2 * B))
    result = jnp.einsum('prc,pcd->prd', paired, turn_matrix, precision=highest)
    return jnp.transpose(result, (1, 0, 2)).reshape(row_count, SLOTS, B)

def reference(snapshot, weights, block_home, plan):
    total_rows = snapshot.shape[0]
    owners = NB // SLOTS
    blocks = jnp.transpose(snapshot.reshape(total_rows, owners, SLOTS, B), (1, 0, 2, 3))
    spread = jnp.take(weights, block_home.astype(jnp.int32), axis=0).reshape(owners, SLOTS, B)
    for round_index in range(ROUNDS):
        ordering = plan[round_index].astype(jnp.int32)
        blocks = jnp.take_along_axis(blocks, ordering[:, None, :, None], axis=2)
        spread = jnp.take_along_axis(spread, ordering[:, :, None], axis=1)
        blocks = lax.map(one_group, (blocks, spread))
        blocks = jnp.stack([jnp.roll(blocks[:, :, 0], 1, axis=0), blocks[:, :, 1], blocks[:, :, 2], jnp.roll(blocks[:, :, 3], -1, axis=0)], axis=2)
        spread = jnp.stack([jnp.roll(spread[:, 0], 1, axis=0), spread[:, 1], spread[:, 2], jnp.roll(spread[:, 3], -1, axis=0)], axis=1)
    result = jnp.transpose(blocks, (1, 0, 2, 3)).reshape(total_rows, NB * B)
    column_norms = jnp.sqrt(lax.optimization_barrier(jnp.sum(result * result, axis=0)))
    return (result, column_norms)
```

```python
import functools

import jax
import jax.numpy as jnp
from jax import lax
from jax.experimental import pallas as pl
from jax.experimental.pallas import tpu as pltpu
from jax.sharding import PartitionSpec as P

MESH = pl.DeviceIdType.MESH
f32, bf16 = jnp.float32, jnp.bfloat16
epsilon = 1e-06
step_size = 4.0
B = 128
W = 2 * B
ROWS = 256
SIDE = 4
N = SIDE**3
T = 8
FAR_FIRST = (2, 1, 3, 0)


def split(x):
    hi = x.astype(bf16)
    return hi, (x - hi.astype(f32)).astype(bf16)


def dot(a, b):
    return jnp.dot(a, b, preferred_element_type=f32)


def dot_t(a, b):
    return lax.dot_general(a, b, (((0,), (0,)), ((), ())), preferred_element_type=f32)


def mm(a, b):
    (ah, al), (bh, bl) = a, b
    return dot(jnp.concatenate([ah, ah, al], axis=1), jnp.concatenate([bh, bl, bh], axis=0))


def mm_t(a, b):
    (ah, al), (bh, bl) = a, b
    return dot_t(jnp.concatenate([ah, ah, al], axis=0), jnp.concatenate([bh, bl, bh], axis=0))


def iotas(n):
    return lax.broadcasted_iota(jnp.int32, (n, n), 0), lax.broadcasted_iota(jnp.int32, (n, n), 1)


def eye_mask():
    r, c = iotas(B)
    return r == c


def diag_row(block, eye):
    return jnp.sum(jnp.where(eye, block, 0.0), axis=0, keepdims=True)


def diag_col(block, eye):
    return jnp.sum(jnp.where(eye, block, 0.0), axis=1, keepdims=True)


def weight_steps(w0, w1):
    eye = eye_mask()
    col = jnp.concatenate([diag_col(jnp.broadcast_to(w, (B, B)), eye) for w in (w0, w1)], axis=0)
    row = jnp.concatenate([w0, w1], axis=1)
    return step_size * (col - row)


def generator(gram, steps):
    eye = eye_mask()
    blocks = (gram[:B, :B], gram[B:, B:])
    inv_row = lax.rsqrt(jnp.concatenate([diag_row(b, eye) for b in blocks], axis=1) + epsilon)
    inv_col = lax.rsqrt(jnp.concatenate([diag_col(b, eye) for b in blocks], axis=0) + epsilon)
    skew = (gram * inv_col * inv_row) * steps
    bound = 1.0 + jnp.max(jnp.sum(jnp.abs(skew), axis=0, keepdims=True), axis=1, keepdims=True)
    return skew * (1.0 / bound)


def newton_schulz(gens, between=()):
    r, c = iotas(W)
    unit = (r == c).astype(f32)
    both = range(len(gens))
    s = [split(g) for g in gens]
    z = [-mm(s[h], s[h]) for h in both]
    x = [unit + gens[h] for h in both]
    for k in range(3):
        zs = [split(z[h]) for h in both]
        u = [mm(zs[h], zs[h]) for h in both]
        x = [x[h] - 0.5 * mm(split(x[h]), zs[h]) for h in both]
        z = [-0.75 * u[h] + 0.25 * mm(split(u[h]), zs[h]) for h in both]
        if k < len(between):
            between[k]()
    zs = [split(z[h]) for h in both]
    u = [mm(zs[h], zs[h]) for h in both]
    tail = [split(0.375 * unit - 0.3125 * z[h] + 0.0625 * u[h]) for h in both]
    last = [mm(split(u[h]), tail[h]) - 0.5 * z[h] for h in both]
    return [x[h] + mm(split(x[h]), split(last[h])) for h in both]


def peers_loop(me, send):
    z, y, x = me // (SIDE * SIDE), lax.rem(me // SIDE, SIDE), lax.rem(me, SIDE)
    slot = 0
    for a in FAR_FIRST:
        for b in FAR_FIRST:
            for c in FAR_FIRST:
                if a or b or c:
                    send(slot, lax.rem(z + a, SIDE) * SIDE * SIDE + lax.rem(y + b, SIDE) * SIDE + lax.rem(x + c, SIDE))
                    slot += 1


def kernel(
    snap, wts, home, plan, out, norms,
    xs, praw, ph, plo, wcur, src0, dsrc, rb0, db0, srcx, rbx, g0, gx, gfull, vbuf, vsend, gd, gdsend,
    rot, obuf, nsend, nrecv, lsem, osem, ssem, rsem, dssem, drsem,
):
    core, me = lax.axis_index("pair"), lax.axis_index("row")
    other = (1 - core, me)
    barrier = pltpu.get_barrier_semaphore()
    loads = [pltpu.make_async_copy(snap.at[:, pl.ds(B * s, B)], xs.at[s], lsem.at[s]) for s in range(4)]
    for load in loads:
        load.start()
    pl.semaphore_signal(barrier, inc=1, device_id=other, device_id_type=MESH)
    peers_loop(me, lambda slot, p: pl.semaphore_signal(barrier, inc=1, device_id=(core, p), device_id_type=MESH))

    remote = []

    def send(source, target, sems, k, device):
        copy = pltpu.make_async_remote_copy(
            source, target, ssem.at[k] if sems is None else sems[0].at[k],
            rsem.at[k] if sems is None else sems[1].at[k], device_id=device, device_id_type=MESH,
        )
        copy.start()
        return copy

    w0 = [wts[pl.ds(home[plan[k]], 1), :] for k in range(4)]
    for k in range(4):
        wcur[4 + k] = jnp.broadcast_to(w0[k], (T, B))
    wcur[1] = wcur[5]
    wcur[2] = wcur[6]
    steps0 = [weight_steps(w0[2 * h], w0[2 * h + 1]) for h in range(2)]

    for load in loads:
        load.wait()
    r, c = iotas(B)
    eye, upper = r == c, r <= c
    for h in range(2):
        for k in range(2):
            praw[1 + h, :, B * k : B * (k + 1)] = xs[plan[2 * h + k]]
        hi, lo = split(praw[1 + h])
        ph[1 + h], plo[1 + h] = hi, lo
        gram = mm_t((hi, lo), (hi, lo))
        src0[pl.ds(2 * h * B, B)] = jnp.where(upper, gram[:B, :B], gram[B:, B:])
        src0[pl.ds((2 * h + 1) * B, B)] = gram[:B, B:]
        dsrc[h : h + 1] = diag_row(gram[B:, B:], eye)

    pl.semaphore_wait(barrier, N)

    def own(rows):
        return pl.ds(pl.multiple_of(rows * T, T), T)

    def scatter(k, source, target):
        peers_loop(me, lambda slot, p: send(source.at[own(p)], target.at[slot], None, k, (core, p)))

    def gather(k, target):
        peers_loop(me, lambda slot, p: send(target.at[own(me)], target.at[own(me)], None, k, (core, p)))

    def wait_all(sems, k, ref):
        pltpu.make_async_copy(ref, ref, sems.at[k]).wait()

    def most(ref):
        return ref.at[pl.ds(0, (N - 1) * T)]

    scatter(0, src0, rb0)
    peers_loop(me, lambda slot, p: send(dsrc, db0.at[slot], None, 1, (core, p)))
    d2d = [
        send(praw.at[1], praw.at[0], (dssem, drsem), 0, other),
        send(praw.at[2], praw.at[3], (dssem, drsem), 1, other),
        send(wcur.at[4], wcur.at[0], (dssem, drsem), 2, other),
        send(wcur.at[7], wcur.at[3], (dssem, drsem), 3, other),
    ]
    for copy in d2d:
        copy.wait_recv()
    for k in (0, 3):
        hi, lo = split(praw[k])
        ph[k], plo[k] = hi, lo
    order = [plan[4 + k] for k in range(4)]
    for h in range(2):
        i, j = order[2 * h], order[2 * h + 1]
        cross = mm_t((ph[i], plo[i]), (ph[j], plo[j]))
        srcx[h, 0:W] = cross[:, :B]
        srcx[h, W : 2 * W] = cross[:, B:]
    scatter(2, srcx.at[0], rbx.at[0])

    wait_all(rsem, 0, rb0)
    wait_all(rsem, 1, db0)
    g0[own(me)] = src0[own(me)] + jnp.sum(rb0[...], axis=0)
    gather(4, g0)
    scatter(3, srcx.at[1], rbx.at[1])
    d22 = dsrc[...] + jnp.sum(db0[...], axis=0)

    def cross_part(h):
        wait_all(rsem, 2 + h, rbx.at[h])
        gx[h, own(me)] = srcx[h, own(me)] + jnp.sum(rbx[h], axis=0)
        gather(5 + h, gx.at[h])

    cross_part(0)
    wait_all(rsem, 4, most(g0))
    gens = []
    for h in range(2):
        tri = g0[2 * h * B : (2 * h + 1) * B]
        a12 = g0[(2 * h + 1) * B : (2 * h + 2) * B]
        tri_t = tri.T
        a11 = jnp.where(upper, tri, tri_t)
        a22 = jnp.where(r > c, tri, jnp.where(eye, d22[h : h + 1], tri_t))
        gram = jnp.concatenate(
            [jnp.concatenate([a11, a12], axis=1), jnp.concatenate([a12.T, a22], axis=1)], axis=0
        )
        gfull[h] = gram
        gens.append(generator(gram, steps0[h]))
    q = newton_schulz(gens, (lambda: None, lambda: cross_part(1)))

    vsend[0], vbuf[1] = q[0][:, :B], q[0][:, B:]
    vbuf[2], vsend[1] = q[1][:, :B], q[1][:, B:]
    vcopies = [
        send(vsend.at[0], vbuf.at[0], (dssem, drsem), 4, other),
        send(vsend.at[1], vbuf.at[3], (dssem, drsem), 5, other),
    ]
    for h in range(2):
        qs = split(q[h])
        hq = split(mm(split(gfull[h]), qs))
        for k in range(2):
            cut = slice(B * k, B * (k + 1))
            block = mm_t(tuple(v[:, cut] for v in qs), tuple(v[:, cut] for v in hq))
            if h == k:
                gdsend[h] = block
            else:
                gd[1 + h] = block
    gcopies = [
        send(gdsend.at[0], gd.at[0], (dssem, drsem), 6, other),
        send(gdsend.at[1], gd.at[3], (dssem, drsem), 7, other),
    ]
    for copy in vcopies:
        copy.wait_recv()
    for h in range(2):
        wait_all(rsem, 5 + h, most(gx.at[h]))
    for k in range(4):
        rot[k] = mm((ph[k], plo[k]), split(vbuf[k]))
    crosses = []
    for h in range(2):
        i, j = order[2 * h], order[2 * h + 1]
        gxh = split(jnp.concatenate([gx[h, 0:W], gx[h, W : 2 * W]], axis=1))
        crosses.append(mm_t(split(vbuf[i]), split(mm(gxh, split(vbuf[j])))))
    for copy in gcopies:
        copy.wait_recv()
    gens = []
    for h in range(2):
        i, j = order[2 * h], order[2 * h + 1]
        gram = jnp.concatenate(
            [
                jnp.concatenate([gd[i], crosses[h]], axis=1),
                jnp.concatenate([crosses[h].T, gd[j]], axis=1),
            ],
            axis=0,
        )
        gfull[h] = gram
        gens.append(generator(gram, weight_steps(wcur[i, 0:1], wcur[j, 0:1])))
    q = newton_schulz(gens)

    stores = []
    for h in range(2):
        i, j = order[2 * h], order[2 * h + 1]
        qs = split(q[h])
        result = mm(split(jnp.concatenate([rot[i], rot[j]], axis=1)), qs)
        for k in range(2):
            obuf[2 * h + k] = result[:, B * k : B * (k + 1)]
            slot = 2 * h + k
            place = out.at[:, pl.ds(B * slot, B)]
            if slot in (0, 3):
                stores.append(send(obuf.at[slot], place, (dssem, drsem), 8 + k, other))
            else:
                copy = pltpu.make_async_copy(obuf.at[slot], place, osem.at[k])
                copy.start()
                stores.append(copy)
        squares = jnp.sum(q[h] * mm(split(gfull[h]), qs), axis=0, keepdims=True)
        root = jnp.sqrt(jnp.maximum(squares, 0.0))
        sent = root[:, h * B : (h + 1) * B]
        kept = root[:, (1 - h) * B : (2 - h) * B]
        nsend[h] = jnp.broadcast_to(sent, (T, B))
        stores.append(send(nsend.at[h], nrecv.at[h], (dssem, drsem), 10 + h, other))
        norms[1 + h : 2 + h] = kept
    for copy in stores:
        copy.wait()
    norms[0:1] = nrecv[0, 0:1]
    norms[3:4] = nrecv[1, 0:1]

    for copy in d2d + vcopies + gcopies:
        copy.wait_send()
    wait_all(ssem, 0, rb0)
    wait_all(ssem, 1, db0)
    for h in range(2):
        wait_all(ssem, 2 + h, rbx.at[h])
        wait_all(ssem, 5 + h, most(gx.at[h]))
    wait_all(ssem, 4, most(g0))


def body(snapshot, weights, block_home, plan):
    vmem = pl.BlockSpec(memory_space=pltpu.VMEM)
    smem = pl.BlockSpec(memory_space=pltpu.SMEM)
    anywhere = pl.BlockSpec(memory_space=pl.ANY)
    V, D = pltpu.VMEM, pltpu.SemaphoreType.DMA
    rotated, norms = pl.pallas_call(
        kernel,
        out_shape=(jax.ShapeDtypeStruct((ROWS, 4 * B), f32), jax.ShapeDtypeStruct((4, B), f32)),
        in_specs=[anywhere, vmem, smem, smem],
        out_specs=(anywhere, vmem),
        scratch_shapes=[
            V((4, ROWS, B), f32),
            V((4, ROWS, W), f32),
            V((4, ROWS, W), bf16),
            V((4, ROWS, W), bf16),
            V((8, T, B), f32),
            V((N * T, B), f32),
            V((2, B), f32),
            V((N - 1, T, B), f32),
            V((N - 1, 2, B), f32),
            V((2, N * T, B), f32),
            V((2, N - 1, T, B), f32),
            V((N * T, B), f32),
            V((2, N * T, B), f32),
            V((2, W, W), f32),
            V((4, W, B), f32),
            V((2, W, B), f32),
            V((4, B, B), f32),
            V((2, B, B), f32),
            V((4, ROWS, B), f32),
            V((4, ROWS, B), f32),
            V((2, T, B), f32),
            V((2, T, B), f32),
            D((4,)),
            D((2,)),
            D((7,)),
            D((7,)),
            D((12,)),
            D((12,)),
        ],
        compiler_params=pltpu.CompilerParams(
            collective_id=0, has_side_effects=True, vmem_limit_bytes=40 << 20
        ),
    )(snapshot, weights, block_home, plan.reshape(-1))
    return rotated, norms.reshape(-1)


def solution(mesh):
    in_specs = (P("row", "pair"), P(), P("pair"), P(None, "pair", None))
    out_specs = (P("row", "pair"), P("pair"))
    return jax.shard_map(body, mesh=mesh, in_specs=in_specs, out_specs=out_specs, check_vma=False)
```

```python
import functools

import jax
import jax.numpy as jnp
from jax import lax
from jax.experimental import pallas as pl
from jax.experimental.pallas import tpu as pltpu
from jax.sharding import PartitionSpec as P

MESH = pl.DeviceIdType.MESH
f32, bf16 = jnp.float32, jnp.bfloat16
epsilon = 1e-06
step_size = 4.0
B = 128
W = 2 * B
ROWS = 256
SIDE = 4
N = SIDE**3
T = 8
FAR_FIRST = (2, 1, 3, 0)
STRIDES = (1, SIDE, SIDE * SIDE)
PLANE = SIDE * SIDE
D = 2
PARTS = ((24, 2), (24, 0), (16, 1))


def split(x):
    hi = x.astype(bf16)
    return hi, (x - hi.astype(f32)).astype(bf16)


def dot(a, b):
    return jnp.dot(a, b, preferred_element_type=f32)


def dot_t(a, b):
    return lax.dot_general(a, b, (((0,), (0,)), ((), ())), preferred_element_type=f32)


def mm(a, b):
    (ah, al), (bh, bl) = a, b
    return dot(jnp.concatenate([ah, ah, al], axis=1), jnp.concatenate([bh, bl, bh], axis=0))


def mm_t(a, b):
    (ah, al), (bh, bl) = a, b
    return dot_t(jnp.concatenate([ah, ah, al], axis=0), jnp.concatenate([bh, bl, bh], axis=0))


def iotas(n):
    return lax.broadcasted_iota(jnp.int32, (n, n), 0), lax.broadcasted_iota(jnp.int32, (n, n), 1)


def eye_mask():
    r, c = iotas(B)
    return r == c


def diag_row(block, eye):
    return jnp.sum(jnp.where(eye, block, 0.0), axis=0, keepdims=True)


def diag_col(block, eye):
    return jnp.sum(jnp.where(eye, block, 0.0), axis=1, keepdims=True)


def weight_steps(w0, w1):
    eye = eye_mask()
    col = jnp.concatenate([diag_col(jnp.broadcast_to(w, (B, B)), eye) for w in (w0, w1)], axis=0)
    row = jnp.concatenate([w0, w1], axis=1)
    return step_size * (col - row)


def generator(gram, steps):
    eye = eye_mask()
    blocks = (gram[:B, :B], gram[B:, B:])
    inv_row = lax.rsqrt(jnp.concatenate([diag_row(b, eye) for b in blocks], axis=1) + epsilon)
    inv_col = lax.rsqrt(jnp.concatenate([diag_col(b, eye) for b in blocks], axis=0) + epsilon)
    skew = (gram * inv_col * inv_row) * steps
    bound = 1.0 + jnp.max(jnp.sum(jnp.abs(skew), axis=0, keepdims=True), axis=1, keepdims=True)
    return skew * (1.0 / bound)


def newton_schulz(gens, between=()):
    r, c = iotas(W)
    unit = (r == c).astype(f32)
    both = range(len(gens))
    s = [split(g) for g in gens]
    z = [-mm(s[h], s[h]) for h in both]
    x = [unit + gens[h] for h in both]
    for k in range(3):
        zs = [split(z[h]) for h in both]
        u = [mm(zs[h], zs[h]) for h in both]
        x = [x[h] - 0.5 * mm(split(x[h]), zs[h]) for h in both]
        z = [-0.75 * u[h] + 0.25 * mm(split(u[h]), zs[h]) for h in both]
        if k < len(between):
            between[k]()
    zs = [split(z[h]) for h in both]
    u = [mm(zs[h], zs[h]) for h in both]
    tail = [split(0.375 * unit - 0.3125 * z[h] + 0.0625 * u[h]) for h in both]
    last = [mm(split(u[h]), tail[h]) - 0.5 * z[h] for h in both]
    return [x[h] + mm(split(x[h]), split(last[h])) for h in both]


def peers_loop(me, send):
    z, y, x = me // (SIDE * SIDE), lax.rem(me // SIDE, SIDE), lax.rem(me, SIDE)
    slot = 0
    for a in FAR_FIRST:
        for b in FAR_FIRST:
            for c in FAR_FIRST:
                if a or b or c:
                    send(slot, lax.rem(z + a, SIDE) * SIDE * SIDE + lax.rem(y + b, SIDE) * SIDE + lax.rem(x + c, SIDE))
                    slot += 1


def digit(me, d):
    return lax.rem(me // STRIDES[d], SIDE)


def plane_loop(me, line, send):
    u, v = (d for d in range(3) if d != line)
    mu, mv = digit(me, u), digit(me, v)
    slot = 0
    for a in FAR_FIRST:
        for b in FAR_FIRST:
            if a or b:
                pu, pv = lax.rem(mu + a, SIDE), lax.rem(mv + b, SIDE)
                send(slot, me + (pu - mu) * STRIDES[u] + (pv - mv) * STRIDES[v], pu * SIDE + pv)
                slot += 1


def plane_place(me, line):
    u, v = (d for d in range(3) if d != line)
    return digit(me, u) * SIDE + digit(me, v)


def kernel(
    snap, wts, home, plan, out, norms,
    xs, praw, ph, plo, wcur, src0, rb0, srcx, rbx0, rbx1, rbx2, line0, line1, line2, g0, gx, gfull,
    vbuf, vsend, gd, gdsend, rot, obuf, nsend, nrecv, lsem, osem, ssem, rsem, dssem, drsem,
):
    rbx, lines = (rbx0, rbx1, rbx2), (line0, line1, line2)
    core, me = lax.axis_index("pair"), lax.axis_index("row")
    other = (1 - core, me)
    barrier = pltpu.get_barrier_semaphore()
    loads = [pltpu.make_async_copy(snap.at[:, pl.ds(B * s, B)], xs.at[s], lsem.at[s]) for s in range(4)]
    for load in loads:
        load.start()
    pl.semaphore_signal(barrier, inc=1, device_id=other, device_id_type=MESH)
    peers_loop(me, lambda slot, p: pl.semaphore_signal(barrier, inc=1, device_id=(core, p), device_id_type=MESH))

    remote = []

    def send(source, target, sems, k, device):
        copy = pltpu.make_async_remote_copy(
            source, target, ssem.at[k] if sems is None else sems[0].at[k],
            rsem.at[k] if sems is None else sems[1].at[k], device_id=device, device_id_type=MESH,
        )
        copy.start()
        return copy

    w0 = [wts[pl.ds(home[plan[0, 0, k]], 1), :] for k in range(4)]
    for k in range(4):
        wcur[4 + k] = jnp.broadcast_to(w0[k], (T, B))
    wcur[1] = wcur[5]
    wcur[2] = wcur[6]
    steps0 = [weight_steps(w0[2 * h], w0[2 * h + 1]) for h in range(2)]

    for load in loads:
        load.wait()
    r, c = iotas(B)
    eye, upper = r == c, r <= c
    for h in range(2):
        for k in range(2):
            praw[1 + h, :, B * k : B * (k + 1)] = xs[plan[0, 0, 2 * h + k]]
        hi, lo = split(praw[1 + h])
        ph[1 + h], plo[1 + h] = hi, lo
        gram = mm_t((hi, lo), (hi, lo))
        packed = jnp.concatenate([jnp.where(upper, gram[:B, :B], gram[B:, B:]), gram[:B, B:]], axis=0)
        src0[h * (N // 2) : (h + 1) * (N // 2), 0:T] = packed.reshape(N // 2, T, B)
        src0[:, T + h : T + h + 1] = jnp.broadcast_to(diag_row(gram[B:, B:], eye), (N, 1, B))

    pl.semaphore_wait(barrier, N)

    def own(rows):
        return pl.ds(pl.multiple_of(rows * T, T), T)


    def wait_all(sems, k, ref):
        pltpu.make_async_copy(ref, ref, sems.at[k]).wait()

    most0 = g0.at[pl.ds(0, (N - 1) * T)]
    bases = (0, PARTS[0][0] * PLANE, (PARTS[0][0] + PARTS[1][0]) * PLANE)

    def piece(part, place):
        rows = PARTS[part][0]
        return pl.ds(pl.multiple_of(bases[part] + place * rows, T), rows)

    def most(part):
        return gx.at[pl.ds(bases[part], (PLANE - 1) * PARTS[part][0])]

    peers_loop(
        me,
        lambda slot, p: send(
            src0.at[p, pl.ds(0, T + D)], rb0.at[slot, pl.ds(0, T + D)], None, 0, (core, p)
        ),
    )
    d2d = [
        send(praw.at[1], praw.at[0], (dssem, drsem), 0, other),
        send(praw.at[2], praw.at[3], (dssem, drsem), 1, other),
        send(wcur.at[4], wcur.at[0], (dssem, drsem), 2, other),
        send(wcur.at[7], wcur.at[3], (dssem, drsem), 3, other),
    ]
    for copy in d2d:
        copy.wait_recv()
    for k in (0, 3):
        hi, lo = split(praw[k])
        ph[k], plo[k] = hi, lo
    order = [plan[1, 0, k] for k in range(4)]
    for h in range(2):
        i, j = order[2 * h], order[2 * h + 1]
        cross = mm_t((ph[i], plo[i]), (ph[j], plo[j]))
        srcx[2 * h * W : (2 * h + 1) * W] = cross[:, :B]
        srcx[(2 * h + 1) * W : (2 * h + 2) * W] = cross[:, B:]
    for part, (rows, line) in enumerate(PARTS):
        plane_loop(
            me,
            line,
            lambda slot, p, place, part=part: send(
                srcx.at[piece(part, place)], rbx[part].at[slot], None, 1 + part, (core, p)
            ),
        )

    arrived = rb0.at[pl.ds(0, N - 1), pl.ds(0, T + D)]
    wait_all(rsem, 0, arrived)
    total = src0[me] + jnp.sum(rb0[...], axis=0)
    g0[own(me)] = total[0:T]
    peers_loop(me, lambda slot, p: send(g0.at[own(me)], g0.at[own(me)], None, 4, (core, p)))
    d22 = total[T : T + D]

    for part, (rows, line) in enumerate(PARTS):
        wait_all(rsem, 1 + part, rbx[part])
        mine = digit(me, line)
        at_mine = lines[part].at[mine]
        lines[part][mine] = srcx[piece(part, plane_place(me, line))] + jnp.sum(rbx[part][...], axis=0)
        for a in range(1, SIDE):
            p = me + (lax.rem(mine + a, SIDE) - mine) * STRIDES[line]
            send(at_mine, at_mine, None, 5 + part, (core, p))

    def cross_gather():
        for part, (rows, line) in enumerate(PARTS):
            wait_all(rsem, 5 + part, lines[part].at[pl.ds(0, SIDE - 1)])
            here = piece(part, plane_place(me, line))
            gx[here] = (lines[part][0] + lines[part][1]) + (lines[part][2] + lines[part][3])
            plane_loop(
                me, line, lambda slot, p, place, part=part: send(gx.at[here], gx.at[here], None, 8 + part, (core, p))
            )

    wait_all(rsem, 4, most0)
    gens = []
    for h in range(2):
        tri = g0[2 * h * B : (2 * h + 1) * B]
        a12 = g0[(2 * h + 1) * B : (2 * h + 2) * B]
        tri_t = tri.T
        a11 = jnp.where(upper, tri, tri_t)
        a22 = jnp.where(r > c, tri, jnp.where(eye, d22[h : h + 1], tri_t))
        gram = jnp.concatenate(
            [jnp.concatenate([a11, a12], axis=1), jnp.concatenate([a12.T, a22], axis=1)], axis=0
        )
        gfull[h] = gram
        gens.append(generator(gram, steps0[h]))
    q = newton_schulz(gens, (cross_gather,))

    vsend[0], vbuf[1] = q[0][:, :B], q[0][:, B:]
    vbuf[2], vsend[1] = q[1][:, :B], q[1][:, B:]
    vcopies = [
        send(vsend.at[0], vbuf.at[0], (dssem, drsem), 4, other),
        send(vsend.at[1], vbuf.at[3], (dssem, drsem), 5, other),
    ]
    for h in range(2):
        qs = split(q[h])
        hq = split(mm(split(gfull[h]), qs))
        for k in range(2):
            cut = slice(B * k, B * (k + 1))
            block = mm_t(tuple(v[:, cut] for v in qs), tuple(v[:, cut] for v in hq))
            if h == k:
                gdsend[h] = block
            else:
                gd[1 + h] = block
    gcopies = [
        send(gdsend.at[0], gd.at[0], (dssem, drsem), 6, other),
        send(gdsend.at[1], gd.at[3], (dssem, drsem), 7, other),
    ]
    for copy in vcopies:
        copy.wait_recv()
    for part in range(3):
        wait_all(rsem, 8 + part, most(part))
    for k in range(4):
        rot[k] = mm((ph[k], plo[k]), split(vbuf[k]))
    crosses = []
    for h in range(2):
        i, j = order[2 * h], order[2 * h + 1]
        gxh = split(
            jnp.concatenate([gx[2 * h * W : (2 * h + 1) * W], gx[(2 * h + 1) * W : (2 * h + 2) * W]], axis=1)
        )
        crosses.append(mm_t(split(vbuf[i]), split(mm(gxh, split(vbuf[j])))))
    for copy in gcopies:
        copy.wait_recv()
    gens = []
    for h in range(2):
        i, j = order[2 * h], order[2 * h + 1]
        gram = jnp.concatenate(
            [
                jnp.concatenate([gd[i], crosses[h]], axis=1),
                jnp.concatenate([crosses[h].T, gd[j]], axis=1),
            ],
            axis=0,
        )
        gfull[h] = gram
        gens.append(generator(gram, weight_steps(wcur[i, 0:1], wcur[j, 0:1])))
    q = newton_schulz(gens)

    stores = []
    for h in range(2):
        i, j = order[2 * h], order[2 * h + 1]
        qs = split(q[h])
        result = mm(split(jnp.concatenate([rot[i], rot[j]], axis=1)), qs)
        for k in range(2):
            obuf[2 * h + k] = result[:, B * k : B * (k + 1)]
            slot = 2 * h + k
            place = out.at[:, pl.ds(B * slot, B)]
            if slot in (0, 3):
                stores.append(send(obuf.at[slot], place, (dssem, drsem), 8 + k, other))
            else:
                copy = pltpu.make_async_copy(obuf.at[slot], place, osem.at[k])
                copy.start()
                stores.append(copy)
        squares = jnp.sum(q[h] * mm(split(gfull[h]), qs), axis=0, keepdims=True)
        root = jnp.sqrt(jnp.maximum(squares, 0.0))
        sent = root[:, h * B : (h + 1) * B]
        kept = root[:, (1 - h) * B : (2 - h) * B]
        nsend[h] = jnp.broadcast_to(sent, (T, B))
        stores.append(send(nsend.at[h], nrecv.at[h], (dssem, drsem), 10 + h, other))
        norms[1 + h : 2 + h] = kept
    for copy in stores:
        copy.wait()
    norms[0:1] = nrecv[0, 0:1]
    norms[3:4] = nrecv[1, 0:1]

    for copy in d2d + vcopies + gcopies:
        copy.wait_send()
    wait_all(ssem, 0, arrived)
    wait_all(ssem, 4, most0)
    for part in range(3):
        wait_all(ssem, 1 + part, rbx[part])
        wait_all(ssem, 5 + part, lines[part].at[pl.ds(0, SIDE - 1)])
        wait_all(ssem, 8 + part, most(part))


def body(snapshot, weights, block_home, plan):
    vmem = pl.BlockSpec(memory_space=pltpu.VMEM)
    smem = pl.BlockSpec(memory_space=pltpu.SMEM)
    anywhere = pl.BlockSpec(memory_space=pl.ANY)
    V, S = pltpu.VMEM, pltpu.SemaphoreType.DMA
    rotated, norms = pl.pallas_call(
        kernel,
        out_shape=(jax.ShapeDtypeStruct((ROWS, 4 * B), f32), jax.ShapeDtypeStruct((4, B), f32)),
        in_specs=[anywhere, vmem, smem, smem],
        out_specs=(anywhere, vmem),
        scratch_shapes=[
            V((4, ROWS, B), f32),
            V((4, ROWS, W), f32),
            V((4, ROWS, W), bf16),
            V((4, ROWS, W), bf16),
            V((8, T, B), f32),
            V((N, 2 * T, B), f32),
            V((N - 1, 2 * T, B), f32),
            V((4 * W, B), f32),
            *[V((PLANE - 1, rows, B), f32) for rows, _ in PARTS],
            *[V((SIDE, rows, B), f32) for rows, _ in PARTS],
            V((N * T, B), f32),
            V((4 * W, B), f32),
            V((2, W, W), f32),
            V((4, W, B), f32),
            V((2, W, B), f32),
            V((4, B, B), f32),
            V((2, B, B), f32),
            V((4, ROWS, B), f32),
            V((4, ROWS, B), f32),
            V((2, T, B), f32),
            V((2, T, B), f32),
            S((4,)),
            S((2,)),
            S((11,)),
            S((11,)),
            S((12,)),
            S((12,)),
        ],
        compiler_params=pltpu.CompilerParams(
            collective_id=0, has_side_effects=True, vmem_limit_bytes=60 << 20
        ),
    )(snapshot, weights, block_home, plan)
    return rotated, norms.reshape(-1)


def solution(mesh):
    in_specs = (P("row", "pair"), P(), P("pair"), P(None, "pair", None))
    out_specs = (P("row", "pair"), P("pair"))
    return jax.shard_map(body, mesh=mesh, in_specs=in_specs, out_specs=out_specs, check_vma=False)
```

```python
import functools

import jax
import jax.numpy as jnp
from jax import lax
from jax.experimental import pallas as pl
from jax.experimental.pallas import tpu as pltpu
from jax.sharding import PartitionSpec as P

MESH = pl.DeviceIdType.MESH
f32, bf16 = jnp.float32, jnp.bfloat16
epsilon = 1e-06
step_size = 4.0
B = 128
W = 2 * B
ROWS = 256
SIDE = 4
N = SIDE**3
T = 8
FAR_FIRST = (2, 1, 3, 0)
STRIDES = (1, SIDE, SIDE * SIDE)
PLANE = SIDE * SIDE
D = 2
PARTS = ((24, 2), (24, 0), (16, 1))


def split(x):
    hi = x.astype(bf16)
    return hi, (x - hi.astype(f32)).astype(bf16)


def dot(a, b):
    return jnp.dot(a, b, preferred_element_type=f32)


def dot_t(a, b):
    return lax.dot_general(a, b, (((0,), (0,)), ((), ())), preferred_element_type=f32)


def halves(f, a):
    cut = a.shape[0] // 2
    return jnp.concatenate([f(a[:cut]), f(a[cut:])], axis=0)


def mm(a, b):
    (ah, al), (bh, bl) = a, b
    right = jnp.concatenate([bh, bl, bh], axis=0)
    return halves(lambda left: dot(left, right), jnp.concatenate([ah, ah, al], axis=1))


def mm1(a, b):
    right = b.astype(bf16)
    return halves(lambda left: dot(left, right), a.astype(bf16))


def mm_t(a, b):
    (ah, al), (bh, bl) = a, b
    return dot_t(jnp.concatenate([ah, ah, al], axis=0), jnp.concatenate([bh, bl, bh], axis=0))


def iotas(n):
    return lax.broadcasted_iota(jnp.int32, (n, n), 0), lax.broadcasted_iota(jnp.int32, (n, n), 1)


def eye_mask():
    r, c = iotas(B)
    return r == c


def diag_row(block, eye):
    return jnp.sum(jnp.where(eye, block, 0.0), axis=0, keepdims=True)


def diag_col(block, eye):
    return jnp.sum(jnp.where(eye, block, 0.0), axis=1, keepdims=True)


def weight_steps(w0, w1):
    eye = eye_mask()
    col = jnp.concatenate([diag_col(jnp.broadcast_to(w, (B, B)), eye) for w in (w0, w1)], axis=0)
    row = jnp.concatenate([w0, w1], axis=1)
    return step_size * (col - row)


def generator(gram, steps):
    eye = eye_mask()
    blocks = (gram[:B, :B], gram[B:, B:])
    inv_row = lax.rsqrt(jnp.concatenate([diag_row(b, eye) for b in blocks], axis=1) + epsilon)
    inv_col = lax.rsqrt(jnp.concatenate([diag_col(b, eye) for b in blocks], axis=0) + epsilon)
    skew = (gram * inv_col * inv_row) * steps
    bound = 1.0 + jnp.max(jnp.sum(jnp.abs(skew), axis=0, keepdims=True), axis=1, keepdims=True)
    return skew * (1.0 / bound)


def newton_schulz(gens, between=()):
    r, c = iotas(W)
    unit = (r == c).astype(f32)
    both = range(len(gens))
    s = [split(g) for g in gens]
    z = [-mm(s[h], s[h]) for h in both]
    x = [unit + gens[h] for h in both]
    for k in range(3):
        zs = [split(z[h]) for h in both]
        u = [mm(zs[h], zs[h]) for h in both]
        x = [x[h] - 0.5 * mm(split(x[h]), zs[h]) for h in both]
        z = [-0.75 * u[h] + 0.25 * mm(split(u[h]), zs[h]) for h in both]
        if k < len(between):
            between[k]()
    u = [mm1(z[h], z[h]) for h in both]
    last = [mm1(u[h], 0.375 * unit - 0.3125 * z[h] + 0.0625 * u[h]) - 0.5 * z[h] for h in both]
    return x, last


def peers_loop(me, send):
    z, y, x = me // (SIDE * SIDE), lax.rem(me // SIDE, SIDE), lax.rem(me, SIDE)
    slot = 0
    for a in FAR_FIRST:
        for b in FAR_FIRST:
            for c in FAR_FIRST:
                if a or b or c:
                    send(slot, lax.rem(z + a, SIDE) * SIDE * SIDE + lax.rem(y + b, SIDE) * SIDE + lax.rem(x + c, SIDE))
                    slot += 1


def digit(me, d):
    return lax.rem(me // STRIDES[d], SIDE)


def plane_loop(me, line, send):
    u, v = (d for d in range(3) if d != line)
    mu, mv = digit(me, u), digit(me, v)
    slot = 0
    for a in FAR_FIRST:
        for b in FAR_FIRST:
            if a or b:
                pu, pv = lax.rem(mu + a, SIDE), lax.rem(mv + b, SIDE)
                send(slot, me + (pu - mu) * STRIDES[u] + (pv - mv) * STRIDES[v], pu * SIDE + pv)
                slot += 1


def plane_place(me, line):
    u, v = (d for d in range(3) if d != line)
    return digit(me, u) * SIDE + digit(me, v)


def kernel(
    snap, wts_in, home_in, plan_in, out, norms,
    wts, home, plan, xs, praw, ph, plo, wcur, src0, rb0, srcx, rbx0, rbx1, rbx2, line0, line1, line2, g0, gx, gfull,
    vbuf, vsend, gd, gdsend, rot, obuf, nsend, nrecv, lsem, ssem, rsem, dssem, drsem,
):
    rbx, lines = (rbx0, rbx1, rbx2), (line0, line1, line2)
    core, me = lax.axis_index("pair"), lax.axis_index("row")
    other = (1 - core, me)
    barrier = pltpu.get_barrier_semaphore()
    loads = [pltpu.make_async_copy(snap.at[:, pl.ds(B * s, B)], xs.at[s], lsem.at[s]) for s in range(4)]
    small = [
        pltpu.make_async_copy(a, b, lsem.at[4 + k])
        for k, (a, b) in enumerate(((wts_in, wts), (home_in, home), (plan_in, plan)))
    ]
    for load in small + loads:
        load.start()
    pl.semaphore_signal(barrier, inc=1, device_id=other, device_id_type=MESH)
    peers_loop(me, lambda slot, p: pl.semaphore_signal(barrier, inc=1, device_id=(core, p), device_id_type=MESH))

    remote = []

    def send(source, target, sems, k, device):
        copy = pltpu.make_async_remote_copy(
            source, target, ssem.at[k] if sems is None else sems[0].at[k],
            rsem.at[k] if sems is None else sems[1].at[k], device_id=device, device_id_type=MESH,
        )
        copy.start()
        return copy

    for load in small:
        load.wait()
    w0 = [wts[pl.ds(home[plan[0, 0, k]], 1), :] for k in range(4)]
    for k in range(4):
        wcur[4 + k] = jnp.broadcast_to(w0[k], (T, B))
    wcur[1] = wcur[5]
    wcur[2] = wcur[6]
    steps0 = [weight_steps(w0[2 * h], w0[2 * h + 1]) for h in range(2)]

    for load in loads:
        load.wait()
    r, c = iotas(B)
    eye, upper = r == c, r <= c
    for h in range(2):
        for k in range(2):
            praw[1 + h, :, B * k : B * (k + 1)] = xs[plan[0, 0, 2 * h + k]]
        hi, lo = split(praw[1 + h])
        ph[1 + h], plo[1 + h] = hi, lo
        gram = mm_t((hi, lo), (hi, lo))
        packed = jnp.concatenate([jnp.where(upper, gram[:B, :B], gram[B:, B:]), gram[:B, B:]], axis=0)
        src0[h * (N // 2) : (h + 1) * (N // 2), 0:T] = packed.reshape(N // 2, T, B)
        src0[:, T + h : T + h + 1] = jnp.broadcast_to(diag_row(gram[B:, B:], eye), (N, 1, B))

    pl.semaphore_wait(barrier, N)

    def own(rows):
        return pl.ds(pl.multiple_of(rows * T, T), T)


    def wait_all(sems, k, ref):
        pltpu.make_async_copy(ref, ref, sems.at[k]).wait()

    most0 = g0.at[pl.ds(0, (N - 1) * T)]
    bases = (0, PARTS[0][0] * PLANE, (PARTS[0][0] + PARTS[1][0]) * PLANE)

    def piece(part, place):
        rows = PARTS[part][0]
        return pl.ds(pl.multiple_of(bases[part] + place * rows, T), rows)

    def most(part):
        return gx.at[pl.ds(bases[part], (PLANE - 1) * PARTS[part][0])]

    peers_loop(
        me,
        lambda slot, p: send(
            src0.at[p, pl.ds(0, T + D)], rb0.at[slot, pl.ds(0, T + D)], None, 0, (core, p)
        ),
    )
    d2d = [
        send(praw.at[1], praw.at[0], (dssem, drsem), 0, other),
        send(praw.at[2], praw.at[3], (dssem, drsem), 1, other),
        send(wcur.at[4], wcur.at[0], (dssem, drsem), 2, other),
        send(wcur.at[7], wcur.at[3], (dssem, drsem), 3, other),
    ]
    for copy in d2d:
        copy.wait_recv()
    for k in (0, 3):
        hi, lo = split(praw[k])
        ph[k], plo[k] = hi, lo
    order = [plan[1, 0, k] for k in range(4)]
    for h in range(2):
        i, j = order[2 * h], order[2 * h + 1]
        cross = mm_t((ph[i], plo[i]), (ph[j], plo[j]))
        srcx[2 * h * W : (2 * h + 1) * W] = cross[:, :B]
        srcx[(2 * h + 1) * W : (2 * h + 2) * W] = cross[:, B:]
    for part, (rows, line) in enumerate(PARTS):
        plane_loop(
            me,
            line,
            lambda slot, p, place, part=part: send(
                srcx.at[piece(part, place)], rbx[part].at[slot], None, 1 + part, (core, p)
            ),
        )

    arrived = rb0.at[pl.ds(0, N - 1), pl.ds(0, T + D)]
    wait_all(rsem, 0, arrived)
    total = src0[me] + jnp.sum(rb0[...], axis=0)
    g0[own(me)] = total[0:T]
    peers_loop(me, lambda slot, p: send(g0.at[own(me)], g0.at[own(me)], None, 4, (core, p)))
    d22 = total[T : T + D]

    for part, (rows, line) in enumerate(PARTS):
        wait_all(rsem, 1 + part, rbx[part])
        mine = digit(me, line)
        at_mine = lines[part].at[mine]
        lines[part][mine] = srcx[piece(part, plane_place(me, line))] + jnp.sum(rbx[part][...], axis=0)
        for a in range(1, SIDE):
            p = me + (lax.rem(mine + a, SIDE) - mine) * STRIDES[line]
            send(at_mine, at_mine, None, 5 + part, (core, p))

    def cross_gather():
        for part, (rows, line) in enumerate(PARTS):
            wait_all(rsem, 5 + part, lines[part].at[pl.ds(0, SIDE - 1)])
            here = piece(part, plane_place(me, line))
            gx[here] = (lines[part][0] + lines[part][1]) + (lines[part][2] + lines[part][3])
            plane_loop(
                me, line, lambda slot, p, place, part=part: send(gx.at[here], gx.at[here], None, 8 + part, (core, p))
            )

    cross_gather()
    wait_all(rsem, 4, most0)
    gens = []
    for h in range(2):
        tri = g0[2 * h * B : (2 * h + 1) * B]
        a12 = g0[(2 * h + 1) * B : (2 * h + 2) * B]
        tri_t = tri.T
        a11 = jnp.where(upper, tri, tri_t)
        a22 = jnp.where(r > c, tri, jnp.where(eye, d22[h : h + 1], tri_t))
        gram = jnp.concatenate(
            [jnp.concatenate([a11, a12], axis=1), jnp.concatenate([a12.T, a22], axis=1)], axis=0
        )
        gfull[h] = gram
        gens.append(generator(gram, steps0[h]))
    x, last = newton_schulz(gens)
    xs3, ls = [split(x[h]) for h in range(2)], [split(last[h]) for h in range(2)]
    hx = [mm(split(gfull[h]), xs3[h]) for h in range(2)]
    q = [x[h] + mm(xs3[h], ls[h]) for h in range(2)]

    vsend[0], vbuf[1] = q[0][:, :B], q[0][:, B:]
    vbuf[2], vsend[1] = q[1][:, :B], q[1][:, B:]
    vcopies = [
        send(vsend.at[0], vbuf.at[0], (dssem, drsem), 4, other),
        send(vsend.at[1], vbuf.at[3], (dssem, drsem), 5, other),
    ]
    for h in range(2):
        hq = split(hx[h] + mm(split(hx[h]), ls[h]))
        qs = split(q[h])
        for k in range(2):
            cut = slice(B * k, B * (k + 1))
            block = mm_t(tuple(v[:, cut] for v in qs), tuple(v[:, cut] for v in hq))
            if h == k:
                gdsend[h] = block
            else:
                gd[1 + h] = block
    gcopies = [
        send(gdsend.at[0], gd.at[0], (dssem, drsem), 6, other),
        send(gdsend.at[1], gd.at[3], (dssem, drsem), 7, other),
    ]

    def turn(k):
        rot[k] = mm((ph[k], plo[k]), split(vbuf[k]))

    turn(1)
    turn(2)
    for copy in vcopies:
        copy.wait_recv()
    for part in range(3):
        wait_all(rsem, 8 + part, most(part))
    crosses = []
    for h in range(2):
        i, j = order[2 * h], order[2 * h + 1]
        gxh = split(
            jnp.concatenate([gx[2 * h * W : (2 * h + 1) * W], gx[(2 * h + 1) * W : (2 * h + 2) * W]], axis=1)
        )
        crosses.append(mm_t(split(vbuf[i]), split(mm(gxh, split(vbuf[j])))))
    for copy in gcopies:
        copy.wait_recv()
    gens = []
    for h in range(2):
        i, j = order[2 * h], order[2 * h + 1]
        gram = jnp.concatenate(
            [
                jnp.concatenate([gd[i], crosses[h]], axis=1),
                jnp.concatenate([crosses[h].T, gd[j]], axis=1),
            ],
            axis=0,
        )
        gfull[h] = gram
        gens.append(generator(gram, weight_steps(wcur[i, 0:1], wcur[j, 0:1])))

    def turn_others():
        turn(0)
        turn(3)

    x, last = newton_schulz(gens, (turn_others,))
    stores = []
    for h in range(2):
        i, j = order[2 * h], order[2 * h + 1]
        xs3, ls = split(x[h]), split(last[h])
        rx = mm(split(jnp.concatenate([rot[i], rot[j]], axis=1)), xs3)
        hx = mm(split(gfull[h]), xs3)
        result = rx + mm(split(rx), ls)
        obuf[h] = result[:, h * B : (h + 1) * B]
        slot = 3 * h
        stores.append(send(obuf.at[h], out.at[:, pl.ds(B * slot, B)], (dssem, drsem), 8 + h, other))
        out[:, (1 + h) * B : (2 + h) * B] = result[:, (1 - h) * B : (2 - h) * B]
        squares = jnp.sum((x[h] + mm(xs3, ls)) * (hx + mm(split(hx), ls)), axis=0, keepdims=True)
        root = jnp.sqrt(jnp.maximum(squares, 0.0))
        nsend[h] = jnp.broadcast_to(root[:, h * B : (h + 1) * B], (T, B))
        stores.append(send(nsend.at[h], nrecv.at[h], (dssem, drsem), 10 + h, other))
        norms[1 + h : 2 + h] = root[:, (1 - h) * B : (2 - h) * B]
    for copy in stores:
        copy.wait()
    norms[0:1] = nrecv[0, 0:1]
    norms[3:4] = nrecv[1, 0:1]

    for copy in d2d + vcopies + gcopies:
        copy.wait_send()
    wait_all(ssem, 0, arrived)
    wait_all(ssem, 4, most0)
    for part in range(3):
        wait_all(ssem, 1 + part, rbx[part])
        wait_all(ssem, 5 + part, lines[part].at[pl.ds(0, SIDE - 1)])
        wait_all(ssem, 8 + part, most(part))


def body(snapshot, weights, block_home, plan):
    vmem = pl.BlockSpec(memory_space=pltpu.VMEM)
    hbm = pl.BlockSpec(memory_space=pltpu.HBM)
    V, S = pltpu.VMEM, pltpu.SemaphoreType.DMA
    rotated, norms = pl.pallas_call(
        kernel,
        out_shape=(jax.ShapeDtypeStruct((ROWS, 4 * B), f32), jax.ShapeDtypeStruct((4, B), f32)),
        in_specs=[hbm] * 4,
        out_specs=(vmem, vmem),
        scratch_shapes=[
            V((8, B), f32),
            pltpu.SMEM((4,), jnp.int32),
            pltpu.SMEM((2, 1, 4), jnp.int32),
            V((4, ROWS, B), f32),
            V((4, ROWS, W), f32),
            V((4, ROWS, W), bf16),
            V((4, ROWS, W), bf16),
            V((8, T, B), f32),
            V((N, 2 * T, B), f32),
            V((N - 1, 2 * T, B), f32),
            V((4 * W, B), f32),
            *[V((PLANE - 1, rows, B), f32) for rows, _ in PARTS],
            *[V((SIDE, rows, B), f32) for rows, _ in PARTS],
            V((N * T, B), f32),
            V((4 * W, B), f32),
            V((2, W, W), f32),
            V((4, W, B), f32),
            V((2, W, B), f32),
            V((4, B, B), f32),
            V((2, B, B), f32),
            V((4, ROWS, B), f32),
            V((2, ROWS, B), f32),
            V((2, T, B), f32),
            V((2, T, B), f32),
            S((7,)),
            S((11,)),
            S((11,)),
            S((12,)),
            S((12,)),
        ],
        compiler_params=pltpu.CompilerParams(
            collective_id=0, has_side_effects=True, vmem_limit_bytes=32 << 20
        ),
    )(*[pltpu.with_memory_space_constraint(a, pltpu.HBM) for a in (snapshot, weights, block_home, plan)])
    return rotated, norms.reshape(-1)


def solution(mesh):
    in_specs = (P("row", "pair"), P(), P("pair"), P(None, "pair", None))
    out_specs = (P("row", "pair"), P("pair"))
    return jax.shard_map(body, mesh=mesh, in_specs=in_specs, out_specs=out_specs, check_vma=False)
```

```python
import functools

import jax
import jax.numpy as jnp
from jax import lax
from jax.experimental import pallas as pl
from jax.experimental.pallas import tpu as pltpu
from jax.sharding import PartitionSpec as P

MESH = pl.DeviceIdType.MESH
f32, bf16 = jnp.float32, jnp.bfloat16
epsilon = 1e-06
step_size = 4.0
B = 128
W = 2 * B
ROWS = 256
SIDE = 4
N = SIDE**3
T = 8
FAR_FIRST = (2, 1, 3, 0)
STRIDES = (1, SIDE, SIDE * SIDE)
PLANE = SIDE * SIDE
D = 2
PARTS = ((24, 2), (24, 0), (16, 1))


def split(x):
    hi = x.astype(bf16)
    return hi, (x - hi.astype(f32)).astype(bf16)


def dot(a, b):
    return jnp.dot(a, b, preferred_element_type=f32)


def halves(f, a):
    cut = a.shape[0] // 2
    return jnp.concatenate([f(a[:cut]), f(a[cut:])], axis=0)


def mm(a, b):
    (ah, al), (bh, bl) = a, b
    right = jnp.concatenate([bh, bl, bh], axis=0)
    return halves(lambda left: dot(left, right), jnp.concatenate([ah, ah, al], axis=1))


def mm1(a, b):
    right = b.astype(bf16)
    return halves(lambda left: dot(left, right), a.astype(bf16))


def split3(x):
    hi, rest = x.astype(bf16), x
    rest = rest - hi.astype(f32)
    mid = rest.astype(bf16)
    return hi, mid, (rest - mid.astype(f32)).astype(bf16)


def mm6(a, b):
    (ah, am, al), (bh, bm, bl) = a, b
    right = jnp.concatenate([bh, bm, bh, bm, bl, bh], axis=0)
    left = jnp.concatenate([ah, ah, am, am, ah, al], axis=1)
    return halves(lambda rows: dot(rows, right), left)


def iotas(n):
    return lax.broadcasted_iota(jnp.int32, (n, n), 0), lax.broadcasted_iota(jnp.int32, (n, n), 1)


def eye_mask():
    r, c = iotas(B)
    return r == c


def diag_row(block, eye):
    return jnp.sum(jnp.where(eye, block, 0.0), axis=0, keepdims=True)


def diag_col(block, eye):
    return jnp.sum(jnp.where(eye, block, 0.0), axis=1, keepdims=True)


def weight_steps(w0, w1):
    eye = eye_mask()
    col = jnp.concatenate([diag_col(jnp.broadcast_to(w, (B, B)), eye) for w in (w0, w1)], axis=0)
    row = jnp.concatenate([w0, w1], axis=1)
    return step_size * (col - row)


def generator(gram, steps):
    eye = eye_mask()
    blocks = (gram[:B, :B], gram[B:, B:])
    inv_row = lax.rsqrt(jnp.concatenate([diag_row(b, eye) for b in blocks], axis=1) + epsilon)
    inv_col = lax.rsqrt(jnp.concatenate([diag_col(b, eye) for b in blocks], axis=0) + epsilon)
    skew = (gram * inv_col * inv_row) * steps
    bound = 1.0 + jnp.max(jnp.sum(jnp.abs(skew), axis=0, keepdims=True), axis=1, keepdims=True)
    return skew * (1.0 / bound)


def newton_schulz(gens, between=()):
    r, c = iotas(W)
    unit = (r == c).astype(f32)
    both = range(len(gens))
    s = [split(g) for g in gens]
    z = [-mm(s[h], s[h]) for h in both]
    x = [unit + gens[h] for h in both]
    for k in range(3):
        zs = [split(z[h]) for h in both]
        u = [mm(zs[h], zs[h]) for h in both]
        x = [x[h] - 0.5 * mm(split(x[h]), zs[h]) for h in both]
        z = [-0.75 * u[h] + 0.25 * mm(split(u[h]), zs[h]) for h in both]
        if k < len(between):
            between[k]()
    u = [mm1(z[h], z[h]) for h in both]
    last = [mm1(u[h], 0.375 * unit - 0.3125 * z[h] + 0.0625 * u[h]) - 0.5 * z[h] for h in both]
    return x, last


def ring_digits(me):
    return [[lax.rem(me // stride + a, SIDE) * stride for a in range(SIDE)] for stride in STRIDES]


def peers_loop(terms, send):
    slot = 0
    for a in FAR_FIRST:
        for b in FAR_FIRST:
            for c in FAR_FIRST:
                if a or b or c:
                    send(slot, terms[2][a] + terms[1][b] + terms[0][c])
                    slot += 1


def digit(me, d):
    return lax.rem(me // STRIDES[d], SIDE)


def plane_loop(terms, line, send):
    u, v = (d for d in range(3) if d != line)
    slot = 0
    for a in FAR_FIRST:
        for b in FAR_FIRST:
            if a or b:
                pu, pv = terms[u][a], terms[v][b]
                place = pu // STRIDES[u] * SIDE + pv // STRIDES[v]
                send(slot, terms[line][0] + pu + pv, place)
                slot += 1


def short_sum(blocks, groups):
    parts = [functools.reduce(lambda a, b: a + b, blocks[k::groups]) for k in range(groups)]
    return functools.reduce(lambda a, b: a + b, parts)


def plane_place(me, line):
    u, v = (d for d in range(3) if d != line)
    return digit(me, u) * SIDE + digit(me, v)


def kernel(
    snap, wts_in, home_in, plan_in, out, norms,
    wts, home, plan, xs, praw, wcur, src0, rb0, srcx, rbx0, rbx1, rbx2, line0, line1, line2, g0, gx, gfull,
    vbuf, vsend, gd, gdsend, rot, obuf, nsend, nrecv, lsem, ssem, rsem, dssem, drsem,
):
    rbx, lines = (rbx0, rbx1, rbx2), (line0, line1, line2)
    core, me = lax.axis_index("pair"), lax.axis_index("row")
    other = (1 - core, me)
    terms = ring_digits(me)
    barrier = pltpu.get_barrier_semaphore()
    loads = [pltpu.make_async_copy(snap.at[:, pl.ds(B * s, B)], xs.at[s], lsem.at[s]) for s in range(4)]
    small = [
        pltpu.make_async_copy(a, b, lsem.at[4 + k])
        for k, (a, b) in enumerate(((wts_in, wts), (home_in, home), (plan_in, plan)))
    ]
    for load in small + loads:
        load.start()
    pl.semaphore_signal(barrier, inc=1, device_id=other, device_id_type=MESH)
    peers_loop(terms, lambda slot, p: pl.semaphore_signal(barrier, inc=1, device_id=(core, p), device_id_type=MESH))

    remote = []

    def send(source, target, sems, k, device):
        copy = pltpu.make_async_remote_copy(
            source, target, ssem.at[k] if sems is None else sems[0].at[k],
            rsem.at[k] if sems is None else sems[1].at[k], device_id=device, device_id_type=MESH,
        )
        copy.start()
        return copy

    for load in small:
        load.wait()
    w0 = [wts[pl.ds(home[plan[0, 0, k]], 1), :] for k in range(4)]
    for k in range(4):
        wcur[4 + k] = jnp.broadcast_to(w0[k], (T, B))
    wcur[1] = wcur[5]
    wcur[2] = wcur[6]
    steps0 = [weight_steps(w0[2 * h], w0[2 * h + 1]) for h in range(2)]

    for load in loads:
        load.wait()
    r, c = iotas(B)
    eye, upper = r == c, r <= c
    for h in range(2):
        for k in range(2):
            praw[1 + h, :, B * k : B * (k + 1)] = xs[plan[0, 0, 2 * h + k]]

    pl.semaphore_wait(barrier, N)
    d2d = [
        send(praw.at[1], praw.at[0], (dssem, drsem), 0, other),
        send(praw.at[2], praw.at[3], (dssem, drsem), 1, other),
        send(wcur.at[4], wcur.at[0], (dssem, drsem), 2, other),
        send(wcur.at[7], wcur.at[3], (dssem, drsem), 3, other),
    ]
    for h in range(2):
        pair = praw[1 + h]
        gram = mm6(split3(pair.T), split3(pair))
        packed = jnp.concatenate([jnp.where(upper, gram[:B, :B], gram[B:, B:]), gram[:B, B:]], axis=0)
        src0[h * (N // 2) : (h + 1) * (N // 2), 0:T] = packed.reshape(N // 2, T, B)
        src0[:, T + h : T + h + 1] = jnp.broadcast_to(diag_row(gram[B:, B:], eye), (N, 1, B))

    def own(rows):
        return pl.ds(pl.multiple_of(rows * T, T), T)


    def wait_all(sems, k, ref):
        pltpu.make_async_copy(ref, ref, sems.at[k]).wait()

    most0 = g0.at[pl.ds(0, (N - 1) * T)]
    bases = (0, PARTS[0][0] * PLANE, (PARTS[0][0] + PARTS[1][0]) * PLANE)

    def piece(part, place):
        rows = PARTS[part][0]
        return pl.ds(pl.multiple_of(bases[part] + place * rows, T), rows)

    def most(part):
        return gx.at[pl.ds(bases[part], (PLANE - 1) * PARTS[part][0])]

    peers_loop(
        terms,
        lambda slot, p: send(
            src0.at[p, pl.ds(0, T + D)], rb0.at[slot, pl.ds(0, T + D)], None, 0, (core, p)
        ),
    )
    for copy in d2d:
        copy.wait_recv()
    order = [plan[1, 0, k] for k in range(4)]
    for h in range(2):
        i, j = order[2 * h], order[2 * h + 1]
        cross = mm6(split3(praw[i].T), split3(praw[j]))
        srcx[2 * h * W : (2 * h + 1) * W] = cross[:, :B]
        srcx[(2 * h + 1) * W : (2 * h + 2) * W] = cross[:, B:]
    for part, (rows, line) in enumerate(PARTS):
        plane_loop(
            terms,
            line,
            lambda slot, p, place, part=part: send(
                srcx.at[piece(part, place)], rbx[part].at[slot], None, 1 + part, (core, p)
            ),
        )

    steps1 = [weight_steps(wcur[order[2 * h], 0:1], wcur[order[2 * h + 1], 0:1]) for h in range(2)]
    arrived = rb0.at[pl.ds(0, N - 1), pl.ds(0, T + D)]
    wait_all(rsem, 0, arrived)
    total = src0[me] + short_sum([rb0[k] for k in range(N - 1)], 9)
    g0[own(me)] = total[0:T]
    peers_loop(terms, lambda slot, p: send(g0.at[own(me)], g0.at[own(me)], None, 4, (core, p)))
    d22 = total[T : T + D]

    for part, (rows, line) in enumerate(PARTS):
        wait_all(rsem, 1 + part, rbx[part])
        mine = digit(me, line)
        at_mine = lines[part].at[mine]
        lines[part][mine] = srcx[piece(part, plane_place(me, line))] + short_sum([rbx[part][k] for k in range(PLANE - 1)], 3)
        for a in range(1, SIDE):
            p = me + (lax.rem(mine + a, SIDE) - mine) * STRIDES[line]
            send(at_mine, at_mine, None, 5 + part, (core, p))

    def cross_gather():
        for part, (rows, line) in enumerate(PARTS):
            wait_all(rsem, 5 + part, lines[part].at[pl.ds(0, SIDE - 1)])
            here = piece(part, plane_place(me, line))
            gx[here] = (lines[part][0] + lines[part][1]) + (lines[part][2] + lines[part][3])
            plane_loop(
                terms, line, lambda slot, p, place, part=part: send(gx.at[here], gx.at[here], None, 8 + part, (core, p))
            )

    cross_gather()
    wait_all(rsem, 4, most0)
    gens = []
    for h in range(2):
        tri = g0[2 * h * B : (2 * h + 1) * B]
        a12 = g0[(2 * h + 1) * B : (2 * h + 2) * B]
        tri_t = tri.T
        a11 = jnp.where(upper, tri, tri_t)
        a22 = jnp.where(r > c, tri, jnp.where(eye, d22[h : h + 1], tri_t))
        gram = jnp.concatenate(
            [jnp.concatenate([a11, a12], axis=1), jnp.concatenate([a12.T, a22], axis=1)], axis=0
        )
        gfull[h] = gram
        gens.append(generator(gram, steps0[h]))
    x, last = newton_schulz(gens)
    xs3, ls = [split(x[h]) for h in range(2)], [split(last[h]) for h in range(2)]
    hx = [mm6(split3(gfull[h]), split3(x[h])) for h in range(2)]
    q = [x[h] + mm(xs3[h], ls[h]) for h in range(2)]

    vsend[0], vbuf[1] = q[0][:, :B], q[0][:, B:]
    vbuf[2], vsend[1] = q[1][:, :B], q[1][:, B:]
    vcopies = [
        send(vsend.at[0], vbuf.at[0], (dssem, drsem), 4, other),
        send(vsend.at[1], vbuf.at[3], (dssem, drsem), 5, other),
    ]
    for h in range(2):
        hq = split3(hx[h] + mm(split(hx[h]), ls[h]))
        qt = split3(q[h].T)
        for k in range(2):
            cut = slice(B * k, B * (k + 1))
            block = mm6(tuple(v[cut] for v in qt), tuple(v[:, cut] for v in hq))
            if h == k:
                gdsend[h] = block
            else:
                gd[1 + h] = block
    gcopies = [
        send(gdsend.at[0], gd.at[0], (dssem, drsem), 6, other),
        send(gdsend.at[1], gd.at[3], (dssem, drsem), 7, other),
    ]

    def turn(k):
        rot[k] = mm(split(praw[k]), split(vbuf[k]))

    for copy in vcopies:
        copy.wait_recv()
    for part in range(3):
        wait_all(rsem, 8 + part, most(part))
    crosses = []
    for h in range(2):
        i, j = order[2 * h], order[2 * h + 1]
        gxh = split3(
            jnp.concatenate([gx[2 * h * W : (2 * h + 1) * W], gx[(2 * h + 1) * W : (2 * h + 2) * W]], axis=1)
        )
        crosses.append(mm6(split3(vbuf[i].T), split3(mm6(gxh, split3(vbuf[j])))))
    for copy in gcopies:
        copy.wait_recv()
    gens = []
    for h in range(2):
        i, j = order[2 * h], order[2 * h + 1]
        gram = jnp.concatenate(
            [
                jnp.concatenate([gd[i], crosses[h]], axis=1),
                jnp.concatenate([crosses[h].T, gd[j]], axis=1),
            ],
            axis=0,
        )
        gfull[h] = gram
        gens.append(generator(gram, steps1[h]))

    def turn_all():
        for k in range(4):
            turn(k)

    x, last = newton_schulz(gens, (turn_all,))
    both = range(2)
    xs3, ls = [split(x[h]) for h in both], [split(last[h]) for h in both]
    rx = [
        mm(split(jnp.concatenate([rot[order[2 * h]], rot[order[2 * h + 1]]], axis=1)), xs3[h]) for h in both
    ]
    hx = [mm(split(gfull[h]), xs3[h]) for h in both]
    result = [rx[h] + mm(split(rx[h]), ls[h]) for h in both]
    stores = []
    for h in both:
        obuf[h] = result[h][:, h * B : (h + 1) * B]
        place = out.at[:, pl.ds(3 * h * B, B)]
        stores.append(send(obuf.at[h], place, (dssem, drsem), 8 + h, other))
    root = []
    for h in both:
        squares = jnp.sum((x[h] + mm(xs3[h], ls[h])) * (hx[h] + mm(split(hx[h]), ls[h])), axis=0, keepdims=True)
        root.append(jnp.sqrt(jnp.maximum(squares, 0.0)))
        nsend[h] = jnp.broadcast_to(root[h][:, h * B : (h + 1) * B], (T, B))
        stores.append(send(nsend.at[h], nrecv.at[h], (dssem, drsem), 10 + h, other))
    for h in both:
        out[:, (1 + h) * B : (2 + h) * B] = result[h][:, (1 - h) * B : (2 - h) * B]
        norms[1 + h : 2 + h] = root[h][:, (1 - h) * B : (2 - h) * B]
    for copy in stores:
        copy.wait()
    norms[0:1] = nrecv[0, 0:1]
    norms[3:4] = nrecv[1, 0:1]

    for copy in d2d + vcopies + gcopies:
        copy.wait_send()
    wait_all(ssem, 0, arrived)
    wait_all(ssem, 4, most0)
    for part in range(3):
        wait_all(ssem, 1 + part, rbx[part])
        wait_all(ssem, 5 + part, lines[part].at[pl.ds(0, SIDE - 1)])
        wait_all(ssem, 8 + part, most(part))


def body(snapshot, weights, block_home, plan):
    vmem = pl.BlockSpec(memory_space=pltpu.VMEM)
    hbm = pl.BlockSpec(memory_space=pltpu.HBM)
    V, S = pltpu.VMEM, pltpu.SemaphoreType.DMA
    rotated, norms = pl.pallas_call(
        kernel,
        out_shape=(jax.ShapeDtypeStruct((ROWS, 4 * B), f32), jax.ShapeDtypeStruct((4, B), f32)),
        in_specs=[hbm] * 4,
        out_specs=(vmem, vmem),
        scratch_shapes=[
            V((8, B), f32),
            pltpu.SMEM((4,), jnp.int32),
            pltpu.SMEM((2, 1, 4), jnp.int32),
            V((4, ROWS, B), f32),
            V((4, ROWS, W), f32),
            V((8, T, B), f32),
            V((N, 2 * T, B), f32),
            V((N - 1, 2 * T, B), f32),
            V((4 * W, B), f32),
            *[V((PLANE - 1, rows, B), f32) for rows, _ in PARTS],
            *[V((SIDE, rows, B), f32) for rows, _ in PARTS],
            V((N * T, B), f32),
            V((4 * W, B), f32),
            V((2, W, W), f32),
            V((4, W, B), f32),
            V((2, W, B), f32),
            V((4, B, B), f32),
            V((2, B, B), f32),
            V((4, ROWS, B), f32),
            V((2, ROWS, B), f32),
            V((2, T, B), f32),
            V((2, T, B), f32),
            S((7,)),
            S((11,)),
            S((11,)),
            S((12,)),
            S((12,)),
        ],
        compiler_params=pltpu.CompilerParams(
            collective_id=0, has_side_effects=True, vmem_limit_bytes=32 << 20
        ),
    )(*[pltpu.with_memory_space_constraint(a, pltpu.HBM) for a in (snapshot, weights, block_home, plan)])
    return rotated, norms.reshape(-1)


def solution(mesh):
    in_specs = (P("row", "pair"), P(), P("pair"), P(None, "pair", None))
    out_specs = (P("row", "pair"), P("pair"))
    return jax.shard_map(body, mesh=mesh, in_specs=in_specs, out_specs=out_specs, check_vma=False)
```

```python
import functools

import jax
import jax.numpy as jnp
from jax import lax
from jax.experimental import pallas as pl
from jax.experimental.pallas import tpu as pltpu
from jax.sharding import PartitionSpec as P

MESH = pl.DeviceIdType.MESH
f32, bf16 = jnp.float32, jnp.bfloat16
epsilon = 1e-06
step_size = 4.0
B = 128
W = 2 * B
ROWS = 256
SIDE = 4
N = SIDE**3
T = 8
FAR_FIRST = (2, 1, 3, 0)
STRIDES = (1, SIDE, SIDE * SIDE)
PLANE = SIDE * SIDE
D = 2
PARTS = ((24, 2), (24, 0), (16, 1))


def split(x):
    hi = x.astype(bf16)
    return hi, (x - hi.astype(f32)).astype(bf16)


def dot(a, b):
    return jnp.dot(a, b, preferred_element_type=f32)


def halves(f, a):
    cut = a.shape[0] // 2
    return jnp.concatenate([f(a[:cut]), f(a[cut:])], axis=0)


def mm(a, b):
    (ah, al), (bh, bl) = a, b
    right = jnp.concatenate([bh, bl, bh], axis=0)
    return halves(lambda left: dot(left, right), jnp.concatenate([ah, ah, al], axis=1))


def mm1(a, b):
    right = b.astype(bf16)
    return halves(lambda left: dot(left, right), a.astype(bf16))


def split3(x):
    hi, rest = x.astype(bf16), x
    rest = rest - hi.astype(f32)
    mid = rest.astype(bf16)
    return hi, mid, (rest - mid.astype(f32)).astype(bf16)


def mm6(a, b):
    (ah, am, al), (bh, bm, bl) = a, b
    right = jnp.concatenate([bh, bm, bh, bm, bl, bh], axis=0)
    left = jnp.concatenate([ah, ah, am, am, ah, al], axis=1)
    return halves(lambda rows: dot(rows, right), left)


def iotas(n):
    return lax.broadcasted_iota(jnp.int32, (n, n), 0), lax.broadcasted_iota(jnp.int32, (n, n), 1)


def eye_mask():
    r, c = iotas(B)
    return r == c


def diag_row(block, eye):
    return jnp.sum(jnp.where(eye, block, 0.0), axis=0, keepdims=True)


def diag_col(block, eye):
    return jnp.sum(jnp.where(eye, block, 0.0), axis=1, keepdims=True)


def weight_steps(w0, w1):
    eye = eye_mask()
    col = jnp.concatenate([diag_col(jnp.broadcast_to(w, (B, B)), eye) for w in (w0, w1)], axis=0)
    row = jnp.concatenate([w0, w1], axis=1)
    return step_size * (col - row)


def generator(gram, steps):
    eye = eye_mask()
    blocks = (gram[:B, :B], gram[B:, B:])
    inv_row = lax.rsqrt(jnp.concatenate([diag_row(b, eye) for b in blocks], axis=1) + epsilon)
    inv_col = lax.rsqrt(jnp.concatenate([diag_col(b, eye) for b in blocks], axis=0) + epsilon)
    skew = (gram * inv_col * inv_row) * steps
    bound = 1.0 + jnp.max(jnp.sum(jnp.abs(skew), axis=0, keepdims=True), axis=1, keepdims=True)
    return skew * (1.0 / bound)


def newton_schulz(gens, between=()):
    r, c = iotas(W)
    unit = (r == c).astype(f32)
    both = range(len(gens))
    s = [split(g) for g in gens]
    z = [-mm(s[h], s[h]) for h in both]
    x = [unit + gens[h] for h in both]
    for k in range(3):
        zs = [split(z[h]) for h in both]
        u = [mm(zs[h], zs[h]) for h in both]
        x = [x[h] - 0.5 * mm(split(x[h]), zs[h]) for h in both]
        z = [-0.75 * u[h] + 0.25 * mm(split(u[h]), zs[h]) for h in both]
        if k < len(between):
            between[k]()
    u = [mm1(z[h], z[h]) for h in both]
    last = [mm1(u[h], 0.375 * unit - 0.3125 * z[h] + 0.0625 * u[h]) - 0.5 * z[h] for h in both]
    return x, last


def ring_digits(me):
    return [[lax.rem(me // stride + a, SIDE) * stride for a in range(SIDE)] for stride in STRIDES]


def peers_loop(terms, send):
    slot = 0
    for a in FAR_FIRST:
        for b in FAR_FIRST:
            for c in FAR_FIRST:
                if a or b or c:
                    send(slot, terms[2][a] + terms[1][b] + terms[0][c])
                    slot += 1


def digit(me, d):
    return lax.rem(me // STRIDES[d], SIDE)


def plane_loop(terms, line, send):
    u, v = (d for d in range(3) if d != line)
    slot = 0
    for a in FAR_FIRST:
        for b in FAR_FIRST:
            if a or b:
                pu, pv = terms[u][a], terms[v][b]
                place = pu // STRIDES[u] * SIDE + pv // STRIDES[v]
                send(slot, terms[line][0] + pu + pv, place)
                slot += 1


def short_sum(blocks, groups):
    parts = [functools.reduce(lambda a, b: a + b, blocks[k::groups]) for k in range(groups)]
    return functools.reduce(lambda a, b: a + b, parts)


def plane_place(me, line):
    u, v = (d for d in range(3) if d != line)
    return digit(me, u) * SIDE + digit(me, v)


def kernel(
    snap, wts_in, home_in, plan_in, out, norms,
    wts, home, plan, xs, praw, wcur, src0, rb0, srcx, rbx0, rbx1, rbx2, line0, line1, line2, g0, gx, gfull,
    vbuf, vsend, gd, gdsend, rot, obuf, nsend, nrecv, lsem, ssem, rsem, dssem, drsem,
):
    rbx, lines = (rbx0, rbx1, rbx2), (line0, line1, line2)
    core, me = lax.axis_index("pair"), lax.axis_index("row")
    other = (1 - core, me)
    terms = ring_digits(me)
    barrier = pltpu.get_barrier_semaphore()
    loads = [pltpu.make_async_copy(snap.at[:, pl.ds(B * s, B)], xs.at[s], lsem.at[s]) for s in range(4)]
    small = [
        pltpu.make_async_copy(a, b, lsem.at[4 + k])
        for k, (a, b) in enumerate(((wts_in, wts), (home_in, home), (plan_in, plan)))
    ]
    for load in small + loads:
        load.start()
    pl.semaphore_signal(barrier, inc=1, device_id=other, device_id_type=MESH)
    peers_loop(terms, lambda slot, p: pl.semaphore_signal(barrier, inc=1, device_id=(core, p), device_id_type=MESH))

    remote = []

    def send(source, target, sems, k, device):
        copy = pltpu.make_async_remote_copy(
            source, target, ssem.at[k] if sems is None else sems[0].at[k],
            rsem.at[k] if sems is None else sems[1].at[k], device_id=device, device_id_type=MESH,
        )
        copy.start()
        return copy

    for load in small:
        load.wait()
    w0 = [wts[pl.ds(home[plan[0, 0, k]], 1), :] for k in range(4)]
    for k in range(4):
        wcur[4 + k] = jnp.broadcast_to(w0[k], (T, B))
    wcur[1] = wcur[5]
    wcur[2] = wcur[6]
    steps0 = [weight_steps(w0[2 * h], w0[2 * h + 1]) for h in range(2)]

    for load in loads:
        load.wait()
    r, c = iotas(B)
    eye, upper = r == c, r <= c
    for h in range(2):
        for k in range(2):
            praw[1 + h, :, B * k : B * (k + 1)] = xs[plan[0, 0, 2 * h + k]]

    pl.semaphore_wait(barrier, N)
    d2d = [
        send(praw.at[1], praw.at[0], (dssem, drsem), 0, other),
        send(praw.at[2], praw.at[3], (dssem, drsem), 1, other),
        send(wcur.at[4], wcur.at[0], (dssem, drsem), 2, other),
        send(wcur.at[7], wcur.at[3], (dssem, drsem), 3, other),
    ]
    for h in range(2):
        pair = praw[1 + h]
        gram = mm6(split3(pair.T), split3(pair))
        packed = jnp.concatenate([jnp.where(upper, gram[:B, :B], gram[B:, B:]), gram[:B, B:]], axis=0)
        src0[h * (N // 2) : (h + 1) * (N // 2), 0:T] = packed.reshape(N // 2, T, B)
        src0[:, T + h : T + h + 1] = jnp.broadcast_to(diag_row(gram[B:, B:], eye), (N, 1, B))

    def own(rows):
        return pl.ds(pl.multiple_of(rows * T, T), T)


    def wait_all(sems, k, ref):
        pltpu.make_async_copy(ref, ref, sems.at[k]).wait()

    most0 = g0.at[pl.ds(0, (N - 1) * T)]
    bases = (0, PARTS[0][0] * PLANE, (PARTS[0][0] + PARTS[1][0]) * PLANE)

    def piece(part, place):
        rows = PARTS[part][0]
        return pl.ds(pl.multiple_of(bases[part] + place * rows, T), rows)

    def most(part):
        return gx.at[pl.ds(bases[part], (PLANE - 1) * PARTS[part][0])]

    peers_loop(
        terms,
        lambda slot, p: send(
            src0.at[p, pl.ds(0, T + D)], rb0.at[slot, pl.ds(0, T + D)], None, 0, (core, p)
        ),
    )
    for copy in d2d:
        copy.wait_recv()
    order = [plan[1, 0, k] for k in range(4)]
    for h in range(2):
        i, j = order[2 * h], order[2 * h + 1]
        cross = mm6(split3(praw[i].T), split3(praw[j]))
        srcx[2 * h * W : (2 * h + 1) * W] = cross[:, :B]
        srcx[(2 * h + 1) * W : (2 * h + 2) * W] = cross[:, B:]
    for part, (rows, line) in enumerate(PARTS):
        plane_loop(
            terms,
            line,
            lambda slot, p, place, part=part: send(
                srcx.at[piece(part, place)], rbx[part].at[slot], None, 1 + part, (core, p)
            ),
        )

    steps1 = [weight_steps(wcur[order[2 * h], 0:1], wcur[order[2 * h + 1], 0:1]) for h in range(2)]
    arrived = rb0.at[pl.ds(0, N - 1), pl.ds(0, T + D)]
    wait_all(rsem, 0, arrived)
    total = src0[me] + short_sum([rb0[k] for k in range(N - 1)], 9)
    g0[own(me)] = total[0:T]
    peers_loop(terms, lambda slot, p: send(g0.at[own(me)], g0.at[own(me)], None, 4, (core, p)))
    d22 = total[T : T + D]

    for part, (rows, line) in enumerate(PARTS):
        wait_all(rsem, 1 + part, rbx[part])
        mine = digit(me, line)
        at_mine = lines[part].at[mine]
        lines[part][mine] = srcx[piece(part, plane_place(me, line))] + short_sum([rbx[part][k] for k in range(PLANE - 1)], 3)
        for a in range(1, SIDE):
            p = me + (lax.rem(mine + a, SIDE) - mine) * STRIDES[line]
            send(at_mine, at_mine, None, 5 + part, (core, p))

    def cross_gather():
        for part, (rows, line) in enumerate(PARTS):
            wait_all(rsem, 5 + part, lines[part].at[pl.ds(0, SIDE - 1)])
            here = piece(part, plane_place(me, line))
            gx[here] = (lines[part][0] + lines[part][1]) + (lines[part][2] + lines[part][3])
            plane_loop(
                terms, line, lambda slot, p, place, part=part: send(gx.at[here], gx.at[here], None, 8 + part, (core, p))
            )

    cross_gather()
    wait_all(rsem, 4, most0)
    gens = []
    for h in range(2):
        tri = g0[2 * h * B : (2 * h + 1) * B]
        a12 = g0[(2 * h + 1) * B : (2 * h + 2) * B]
        tri_t = tri.T
        a11 = jnp.where(upper, tri, tri_t)
        a22 = jnp.where(r > c, tri, jnp.where(eye, d22[h : h + 1], tri_t))
        gram = jnp.concatenate(
            [jnp.concatenate([a11, a12], axis=1), jnp.concatenate([a12.T, a22], axis=1)], axis=0
        )
        gfull[h] = gram
        gens.append(generator(gram, steps0[h]))
    x, last = newton_schulz(gens)
    xs3, ls = [split(x[h]) for h in range(2)], [split(last[h]) for h in range(2)]
    hx = [mm6(split3(gfull[h]), split3(x[h])) for h in range(2)]
    q = [x[h] + mm(xs3[h], ls[h]) for h in range(2)]

    vsend[0], vbuf[1] = q[0][:, :B], q[0][:, B:]
    vbuf[2], vsend[1] = q[1][:, :B], q[1][:, B:]
    vcopies = [
        send(vsend.at[0], vbuf.at[0], (dssem, drsem), 4, other),
        send(vsend.at[1], vbuf.at[3], (dssem, drsem), 5, other),
    ]
    for h in range(2):
        hq = split3(hx[h] + mm(split(hx[h]), ls[h]))
        qt = split3(q[h].T)
        for k in range(2):
            cut = slice(B * k, B * (k + 1))
            block = mm6(tuple(v[cut] for v in qt), tuple(v[:, cut] for v in hq))
            if h == k:
                gdsend[h] = block
            else:
                gd[1 + h] = block
    gcopies = [
        send(gdsend.at[0], gd.at[0], (dssem, drsem), 6, other),
        send(gdsend.at[1], gd.at[3], (dssem, drsem), 7, other),
    ]

    def turn(k):
        rot[k] = mm(split(praw[k]), split(vbuf[k]))

    turn(1)
    turn(2)
    for copy in vcopies:
        copy.wait_recv()
    for part in range(3):
        wait_all(rsem, 8 + part, most(part))
    crosses = []
    for h in range(2):
        i, j = order[2 * h], order[2 * h + 1]
        gxh = split3(
            jnp.concatenate([gx[2 * h * W : (2 * h + 1) * W], gx[(2 * h + 1) * W : (2 * h + 2) * W]], axis=1)
        )
        crosses.append(mm6(split3(vbuf[i].T), split3(mm6(gxh, split3(vbuf[j])))))
    for copy in gcopies:
        copy.wait_recv()
    gens = []
    for h in range(2):
        i, j = order[2 * h], order[2 * h + 1]
        gram = jnp.concatenate(
            [
                jnp.concatenate([gd[i], crosses[h]], axis=1),
                jnp.concatenate([crosses[h].T, gd[j]], axis=1),
            ],
            axis=0,
        )
        gfull[h] = gram
        gens.append(generator(gram, steps1[h]))

    def turn_all():
        for k in (0, 3):
            turn(k)

    x, last = newton_schulz(gens, (turn_all,))
    both = range(2)
    xs3, ls = [split(x[h]) for h in both], [split(last[h]) for h in both]
    rx = [
        mm(split(jnp.concatenate([rot[order[2 * h]], rot[order[2 * h + 1]]], axis=1)), xs3[h]) for h in both
    ]
    hx = [mm(split(gfull[h]), xs3[h]) for h in both]
    result = [rx[h] + mm(split(rx[h]), ls[h]) for h in both]
    stores = []
    for h in both:
        obuf[h] = result[h][:, h * B : (h + 1) * B]
        place = out.at[:, pl.ds(3 * h * B, B)]
        stores.append(send(obuf.at[h], place, (dssem, drsem), 8 + h, other))
    root = []
    for h in both:
        squares = jnp.sum((x[h] + mm(xs3[h], ls[h])) * (hx[h] + mm(split(hx[h]), ls[h])), axis=0, keepdims=True)
        root.append(jnp.sqrt(jnp.maximum(squares, 0.0)))
        nsend[h] = jnp.broadcast_to(root[h][:, h * B : (h + 1) * B], (T, B))
        stores.append(send(nsend.at[h], nrecv.at[h], (dssem, drsem), 10 + h, other))
    for h in both:
        out[:, (1 + h) * B : (2 + h) * B] = result[h][:, (1 - h) * B : (2 - h) * B]
        norms[1 + h : 2 + h] = root[h][:, (1 - h) * B : (2 - h) * B]
    for copy in stores:
        copy.wait()
    norms[0:1] = nrecv[0, 0:1]
    norms[3:4] = nrecv[1, 0:1]

    for copy in d2d + vcopies + gcopies:
        copy.wait_send()
    wait_all(ssem, 0, arrived)
    wait_all(ssem, 4, most0)
    for part in range(3):
        wait_all(ssem, 1 + part, rbx[part])
        wait_all(ssem, 5 + part, lines[part].at[pl.ds(0, SIDE - 1)])
        wait_all(ssem, 8 + part, most(part))


def body(snapshot, weights, block_home, plan):
    vmem = pl.BlockSpec(memory_space=pltpu.VMEM)
    hbm = pl.BlockSpec(memory_space=pltpu.HBM)
    V, S = pltpu.VMEM, pltpu.SemaphoreType.DMA
    rotated, norms = pl.pallas_call(
        kernel,
        out_shape=(jax.ShapeDtypeStruct((ROWS, 4 * B), f32), jax.ShapeDtypeStruct((4, B), f32)),
        in_specs=[hbm] * 4,
        out_specs=(vmem, vmem),
        scratch_shapes=[
            V((8, B), f32),
            pltpu.SMEM((4,), jnp.int32),
            pltpu.SMEM((2, 1, 4), jnp.int32),
            V((4, ROWS, B), f32),
            V((4, ROWS, W), f32),
            V((8, T, B), f32),
            V((N, 2 * T, B), f32),
            V((N - 1, 2 * T, B), f32),
            V((4 * W, B), f32),
            *[V((PLANE - 1, rows, B), f32) for rows, _ in PARTS],
            *[V((SIDE, rows, B), f32) for rows, _ in PARTS],
            V((N * T, B), f32),
            V((4 * W, B), f32),
            V((2, W, W), f32),
            V((4, W, B), f32),
            V((2, W, B), f32),
            V((4, B, B), f32),
            V((2, B, B), f32),
            V((4, ROWS, B), f32),
            V((2, ROWS, B), f32),
            V((2, T, B), f32),
            V((2, T, B), f32),
            S((7,)),
            S((11,)),
            S((11,)),
            S((12,)),
            S((12,)),
        ],
        compiler_params=pltpu.CompilerParams(
            collective_id=0, has_side_effects=True, vmem_limit_bytes=32 << 20
        ),
    )(*[pltpu.with_memory_space_constraint(a, pltpu.HBM) for a in (snapshot, weights, block_home, plan)])
    return rotated, norms.reshape(-1)


def solution(mesh):
    in_specs = (P("row", "pair"), P(), P("pair"), P(None, "pair", None))
    out_specs = (P("row", "pair"), P("pair"))
    return jax.shard_map(body, mesh=mesh, in_specs=in_specs, out_specs=out_specs, check_vma=False)
```
